256 devices in a mesh: dp: 2 (over core), ctx: 128 (over x, z, y).
Axes of the slice: x: 4, y: 4, z: 8, core: 2. Of those that a mesh axis runs over, the one named last changes fastest.
Arguments:
- queries: bfloat16 [2, 16384, 2048], P('dp', 'ctx'), may hold values from -6 to 6
- keys: bfloat16 [2, 16384, 2048], P('dp', 'ctx'), may hold values from -6 to 6
- values: bfloat16 [2, 16384, 2048], P('dp', 'ctx'), may hold values from -6 to 6
- doc_ids: int32 [2, 256], P('dp', 'ctx'), may hold values from 0 to 7, never falling along the last dimension, each value on 1 to 64 neighbouring positions
- feat_weight: bfloat16 [128, 160], replicated, may hold values from -0.5 to 0.5
- out_grad: bfloat16 [2, 16384, 2048], P('dp', 'ctx'), may hold values from -6 to 6
Outputs:
- out: float32 [2, 16384, 2048], P('dp', 'ctx')
- query_grad: float32 [2, 16384, 2048], P('dp', 'ctx')
- key_grad: float32 [2, 16384, 2048], P('dp', 'ctx')
- value_grad: float32 [2, 16384, 2048], P('dp', 'ctx')
- new_weight: float32 [128, 160], replicated
The draws below stay inside these ranges and needn't reach their ends.
Inputs may be any that keep to these rules, and one draw needn't show every extreme that they name: `doc_ids`: along each sequence the ids never fall; every id names one run of 1 to 64 blocks, and one run has exactly 64 blocks.
All inputs are finite; a program needn't handle non-finite values.
Results may differ from the reference program's by a relative error of at most 0.015.
Values sent between devices are 32-bit elements; how exact they have to be, the bound alone decides.
No kernel may reach another device: no remote copies, remote signals or barrier semaphores. Data moves between devices by JAX's collectives and lax.ppermute only.
A program may use at most 64 MiB of HBM per device.

```python
import math
import jax
import jax.numpy as jnp
import numpy as np
from jax import lax

H = 16
DH = 128
F = 160
BLOCK = 64
DOCS = 8
T_DEV = 128
SEQS = 2
LEN = 16384
BLOCKS = 256
MOST = 64
N_CTX = 128


def shard_levels(own_key, extent, pieces, smallest, largest):
    def one(dim, shards_of):
        draws = jax.random.uniform(jax.random.fold_in(jax.random.fold_in(own_key, 6), dim), (shards_of,), jnp.float32, smallest / len(pieces), largest / len(pieces))
        return jnp.repeat(jnp.exp(draws), extent[dim] // shards_of).reshape((-1,) + (1,) * (len(extent) - dim - 1))

    factor_of = one(*pieces[0])
    for cut in pieces[1:]:
        factor_of = factor_of * one(*cut)
    return factor_of


def split_up(number_of, total, most, skew):
    portions = [(1 << 20) // math.isqrt(standing ** skew) + 1 for standing in range(2, number_of + 1)]
    surplus, counts = total - most - (number_of - 1), [1] * (number_of - 1)
    while surplus > 0:
        candidates = [i for i in range(number_of - 1) if counts[i] < most]
        whole, budget = sum([portions[i] for i in candidates]), surplus
        for i in candidates:
            extra = min(most - counts[i], max(1, budget * portions[i] // whole), surplus)
            counts[i] = counts[i] + extra
            surplus = surplus - extra
    return np.array([most] + counts)


def uneven_parts(stream_key, count, total, reach, slope):
    if count == 2:
        one = jax.random.randint(stream_key, (), max(1, total - reach), min(reach, total - 1) + 1)
        return jnp.stack([one, total - one])
    tallies = jnp.asarray(split_up(count, total, reach, slope), jnp.int32)
    pairs = (count - 1) // 2
    donor, receiver = tallies[1:1 + 2 * pairs:2], tallies[2:2 + 2 * pairs:2]
    slack = jnp.minimum(donor - 1, reach - receiver)
    moved = jax.random.randint(jax.random.fold_in(stream_key, 1), (pairs,), 0, 1 << 20) % (slack + 1)
    tallies = tallies.at[1:1 + 2 * pairs:2].set(donor - moved).at[2:2 + 2 * pairs:2].set(receiver + moved)
    return tallies[jax.random.permutation(jax.random.fold_in(stream_key, 2), count)]


def centred(rng, dims, spread, limit, cuts=(), dtype=jnp.bfloat16):
    drawn = spread * jax.random.normal(rng, dims, jnp.float32)
    if cuts:
        drawn = drawn * shard_levels(rng, dims, cuts, -0.22, 0.18)
    return jnp.clip(drawn, -limit, limit).astype(dtype)


def setup_inputs(seed: int = 0) -> dict:
    splits = jax.random.split(jax.random.key(seed), 7)
    return {
        "queries": centred(splits[0], (SEQS, LEN, H * DH), 1.0, 6.0, ((0, 2), (1, 128))),
        "keys": centred(splits[1], (SEQS, LEN, H * DH), 1.0, 6.0, ((0, 2), (1, 128))),
        "values": centred(splits[2], (SEQS, LEN, H * DH), 1.0, 6.0, ((0, 2), (1, 128))),
        "doc_ids": jax.vmap(lambda own: jnp.searchsorted(jnp.cumsum(uneven_parts(own, DOCS, BLOCKS, MOST, 0)), jnp.arange(BLOCKS), side="right"))(jax.random.split(splits[3], SEQS)).reshape((SEQS, BLOCKS)).astype(jnp.int32),
        "feat_weight": centred(splits[4], (DH, F), DH ** -0.5, 0.5),
        "out_grad": centred(splits[5], (SEQS, LEN, H * DH), 1.0, 6.0, ((0, 2), (1, 128))),
    }


HIGH = lax.Precision.HIGHEST
RATE = 0.5
EPSILON = 1e-06

def features(proj):
    return (1.0 + proj + 0.5 * proj * proj).astype(jnp.bfloat16)

def section_local(query3, key3, docs, weight):
    weight_f = weight.astype(jnp.float32)
    proj_q = jnp.einsum('thd,df->thf', query3.astype(jnp.float32), weight_f, precision=HIGH)
    proj_k = jnp.einsum('thd,df->thf', key3.astype(jnp.float32), weight_f, precision=HIGH)
    feat_q = features(proj_q)
    feat_k = features(proj_k)
    order = jnp.arange(docs.shape[0])
    mask = jnp.logical_and(order[None, :] <= order[:, None], docs[None, :] == docs[:, None]).astype(jnp.float32)
    raw = jnp.einsum('thf,shf->hts', feat_q.astype(jnp.float32), feat_k.astype(jnp.float32), precision=HIGH)
    probs = (raw * mask[None]).astype(jnp.bfloat16)
    return (proj_q, proj_k, feat_q, feat_k, mask, probs)

def section_forward(query3, key3, value3, docs, weight, state_in, norm_in, pre_end):
    proj_q, proj_k, feat_q, feat_k, mask, probs = section_local(query3, key3, docs, weight)
    feat_qf = feat_q.astype(jnp.float32)
    value_f = value3.astype(jnp.float32)
    in_mask = (docs == pre_end).astype(jnp.float32)
    probs_f = probs.astype(jnp.float32)
    num_local = jnp.einsum('hts,shd->thd', probs_f, value_f, precision=HIGH)
    den_local = lax.optimization_barrier(jnp.sum(probs_f, axis=2)).T
    den = den_local + jnp.einsum('thf,hf->th', feat_qf, norm_in, precision=HIGH) * in_mask[:, None]
    out = (num_local + jnp.einsum('thf,hfd->thd', feat_qf, state_in, precision=HIGH) * in_mask[:, None, None]) / den[:, :, None]
    return (proj_q, proj_k, feat_q, feat_k, mask, probs, in_mask, den, out)

def one_sequence(queries, keys, values, doc_ids, weight, out_grad):
    query4 = queries.reshape(N_CTX, T_DEV, H, DH)
    key4 = keys.reshape(N_CTX, T_DEV, H, DH)
    value4 = values.reshape(N_CTX, T_DEV, H, DH)
    grad4 = out_grad.reshape(N_CTX, T_DEV, H, DH)
    docs4 = jnp.repeat(doc_ids, BLOCK).astype(jnp.int32).reshape(N_CTX, T_DEV)

    def forward_step(carry, items):
        state, norm, end = carry
        query3, key3, value3, docs = items
        proj_q, proj_k, feat_q, feat_k, mask, probs = section_local(query3, key3, docs, weight)
        tail_mask = (docs == docs[-1]).astype(jnp.float32)
        feat_kf = feat_k.astype(jnp.float32)
        tail_state = jnp.einsum('thf,thd->hfd', feat_kf * tail_mask[:, None, None], value3.astype(jnp.float32), precision=HIGH)
        tail_norm = jnp.einsum('thf,t->hf', feat_kf, tail_mask, precision=HIGH)
        joined = docs[-1] == end
        new_state = tail_state + jnp.where(joined, state, jnp.zeros_like(state))
        new_norm = tail_norm + jnp.where(joined, norm, jnp.zeros_like(norm))
        return ((new_state, new_norm, docs[-1].astype(jnp.int32)), (state, norm, end))
    start = (jnp.zeros((H, F, DH), jnp.float32), jnp.zeros((H, F), jnp.float32), jnp.array(-1, jnp.int32))
    _, (states, norms, ends) = lax.scan(forward_step, start, (query4, key4, value4, docs4))

    def backward_step(carry, items):
        adjoint, adjoint_norm, key_doc, grad_total = carry
        query3, key3, value3, grad3, docs, state_in, norm_in, pre_end = items
        proj_q, proj_k, feat_q, feat_k, mask, probs, in_mask, den, out = section_forward(query3, key3, value3, docs, weight, state_in, norm_in, pre_end)
        feat_qf = feat_q.astype(jnp.float32)
        feat_kf = feat_k.astype(jnp.float32)
        value_f = value3.astype(jnp.float32)
        grad_f = grad3.astype(jnp.float32)
        scaled = grad_f / den[:, :, None]
        scaled_b = scaled.astype(jnp.bfloat16).astype(jnp.float32)
        drift = -lax.optimization_barrier(jnp.sum(grad_f * out, axis=2)) / den
        dscore = jnp.einsum('thd,shd->hts', scaled_b, value_f, precision=HIGH) + drift.T[:, :, None]
        dprobs = (dscore * mask[None]).astype(jnp.bfloat16).astype(jnp.float32)
        out_mask = (docs == key_doc).astype(jnp.float32)
        grad_fq = jnp.einsum('hts,shf->thf', dprobs, feat_kf, precision=HIGH) + (jnp.einsum('hfd,thd->thf', state_in, scaled, precision=HIGH) + norm_in[None] * drift[:, :, None]) * in_mask[:, None, None]
        grad_fk = jnp.einsum('hts,thf->shf', dprobs, feat_qf, precision=HIGH) + (jnp.einsum('hfd,shd->shf', adjoint, value_f, precision=HIGH) + adjoint_norm[None]) * out_mask[:, None, None]
        value_grad = jnp.einsum('hts,thd->shd', probs.astype(jnp.float32), scaled_b, precision=HIGH) + jnp.einsum('shf,hfd->shd', feat_kf, adjoint, precision=HIGH) * out_mask[:, None, None]
        grad_pq = (grad_fq * (1.0 + proj_q)).astype(jnp.bfloat16).astype(jnp.float32)
        grad_pk = (grad_fk * (1.0 + proj_k)).astype(jnp.bfloat16).astype(jnp.float32)
        weight_f = weight.astype(jnp.float32)
        query_grad = jnp.einsum('thf,df->thd', grad_pq, weight_f, precision=HIGH)
        key_grad = jnp.einsum('thf,df->thd', grad_pk, weight_f, precision=HIGH)
        grad_here = jnp.einsum('thd,thf->df', query3.astype(jnp.float32), grad_pq, precision=HIGH) + jnp.einsum('thd,thf->df', key3.astype(jnp.float32), grad_pk, precision=HIGH)
        head_mask = (docs == docs[0]).astype(jnp.float32)
        head_state = jnp.einsum('thf,thd->hfd', feat_qf * head_mask[:, None, None], scaled, precision=HIGH)
        head_norm = jnp.einsum('thf,th->hf', feat_qf * head_mask[:, None, None], drift, precision=HIGH)
        joined = docs[0] == key_doc
        new_adjoint = head_state + jnp.where(joined, adjoint, jnp.zeros_like(adjoint))
        new_norm = head_norm + jnp.where(joined, adjoint_norm, jnp.zeros_like(adjoint_norm))
        carry = (new_adjoint, new_norm, docs[0].astype(jnp.int32), grad_total + grad_here)
        return (carry, (out, query_grad, key_grad, value_grad))
    start = (jnp.zeros((H, F, DH), jnp.float32), jnp.zeros((H, F), jnp.float32), jnp.array(-1, jnp.int32), jnp.zeros((DH, F), jnp.float32))
    final, results = lax.scan(backward_step, start, (query4, key4, value4, grad4, docs4, states, norms, ends), reverse=True)
    shaped = tuple((item.reshape(LEN, H * DH) for item in results))
    return (shaped, final[3])

def reference(queries, keys, values, doc_ids, feat_weight, out_grad):
    outs = []
    weight_grad = jnp.zeros((DH, F), jnp.float32)
    for index in range(SEQS):
        shaped, grad_part = one_sequence(queries[index], keys[index], values[index], doc_ids[index], feat_weight, out_grad[index])
        outs.append(shaped)
        weight_grad = weight_grad + grad_part
    stacked = tuple((jnp.stack([item[position] for item in outs]) for position in range(4)))
    scale = lax.rsqrt(jnp.mean(weight_grad * weight_grad) + EPSILON)
    new_weight = feat_weight.astype(jnp.float32) - RATE * weight_grad * scale
    return (stacked[0], stacked[1], stacked[2], stacked[3], new_weight)
```

```python
import jax
import jax.numpy as jnp
from jax import lax
from jax.experimental import pallas as pl
from jax.experimental.pallas import tpu as pltpu
from jax.sharding import PartitionSpec as P

H = 16
DH = 128
F = 160
BLOCK = 64
T = 128
RATE = 0.5
EPSILON = 1e-06
GROUP = 8
PAIR = H // GROUP
REACH = 4
TAIL = PAIR * F
ROWS = TAIL + 8
FIRST = TAIL + 2 * PAIR
LAST = FIRST + 1

F32 = jnp.float32
BF16 = jnp.bfloat16


def dot(a, b, over):
    return lax.dot_general(a, b, (((over[0],), (over[1],)), ((), ())), preferred_element_type=F32)


def head_rows(d_ref):
    limit = jnp.where(d_ref[0, 0] == d_ref[0, 1], T, BLOCK)
    return lax.broadcasted_iota(jnp.int32, (T, 1), 0) < limit


def tail_rows(d_ref):
    limit = jnp.where(d_ref[0, 0] == d_ref[0, 1], 0, BLOCK)
    return lax.broadcasted_iota(jnp.int32, (T, 1), 0) >= limit


def pair_mask(d_ref):
    rows = lax.broadcasted_iota(jnp.int32, (T, T), 0)
    cols = lax.broadcasted_iota(jnp.int32, (T, T), 1)
    start = jnp.where(d_ref[0, 0] == d_ref[0, 1], 0, BLOCK)
    return jnp.logical_and(cols <= rows, jnp.logical_or(rows < start, cols >= start) | (rows < BLOCK))


def small_rows(d_ref, norms):
    rows = []
    for norm in norms:
        rows.append(norm[:, :DH])
        rows.append(jnp.concatenate([norm[:, DH:], jnp.zeros((1, 2 * DH - F), F32)], axis=1))
    rows.append(jnp.full((1, DH), d_ref[0, 0].astype(F32)))
    rows.append(jnp.full((1, DH), d_ref[0, 1].astype(F32)))
    rows.append(jnp.zeros((ROWS - LAST - 1, DH), F32))
    return jnp.concatenate(rows, axis=0)


def norm_row(s_ref, a):
    start = TAIL + 2 * a
    return jnp.concatenate(
        [s_ref[0, start : start + 1, :], s_ref[0, start + 1 : start + 2, : F - DH]], axis=1
    )


def cols(a):
    return slice(a * DH, (a + 1) * DH)


def key_kernel(d_ref, k_ref, v_ref, w_ref, y_ref, fk_ref, ok_ref):
    tail = tail_rows(d_ref)
    norms = []
    for a in range(PAIR):
        proj = dot(k_ref[:, cols(a)], w_ref[...], (1, 0))
        feat = 1.0 + proj + 0.5 * proj * proj
        feat_b = feat.astype(BF16)
        fk_ref[a] = feat_b
        ok_ref[a] = 1.0 + proj
        kept = jnp.where(tail, feat_b.astype(F32), 0.0)
        y_ref[0, a * F : (a + 1) * F, :] = dot(kept.astype(BF16), v_ref[:, cols(a)], (0, 0))
        norms.append(jnp.sum(kept, axis=0, keepdims=True))
    y_ref[0, TAIL:, :] = small_rows(d_ref, norms)


def local_kernel(d_ref, q_ref, v_ref, w_ref, fk_ref, fq_ref, oq_ref, pr_ref, num_ref, den_ref):
    mask = pair_mask(d_ref)
    for a in range(PAIR):
        proj = dot(q_ref[:, cols(a)], w_ref[...], (1, 0))
        feat_b = (1.0 + proj + 0.5 * proj * proj).astype(BF16)
        fq_ref[a] = feat_b
        oq_ref[a] = 1.0 + proj
        raw = dot(feat_b, fk_ref[a], (1, 1))
        probs = jnp.where(mask, raw, 0.0).astype(BF16)
        pr_ref[a] = probs
        num_ref[:, cols(a)] = dot(probs, v_ref[:, cols(a)], (1, 0))
        den_ref[a] = jnp.sum(probs.astype(F32), axis=1, keepdims=True)


def out_kernel(d_ref, fq_ref, num_ref, den_ref, g_ref, s_ref, y_ref, out_ref, sc_ref, dr_ref):
    head = head_rows(d_ref)
    norms = []
    for a in range(PAIR):
        feat = fq_ref[a]
        kept = jnp.where(head, feat.astype(F32), 0.0)
        kept_b = kept.astype(BF16)
        norm = norm_row(s_ref, a)
        den = den_ref[a] + jnp.sum(kept * norm, axis=1, keepdims=True)
        inv = 1.0 / den
        state = s_ref[0, a * F : (a + 1) * F, :].astype(BF16)
        grad = g_ref[:, cols(a)].astype(F32)
        out = (num_ref[:, cols(a)] + dot(kept_b, state, (1, 0))) * inv
        out_ref[:, cols(a)] = out
        scaled = (grad * inv).astype(BF16)
        sc_ref[:, cols(a)] = scaled
        drift = -jnp.sum(grad * out, axis=1, keepdims=True) * inv
        dr_ref[a] = drift
        y_ref[0, a * F : (a + 1) * F, :] = dot(kept_b, scaled, (0, 0))
        norms.append(jnp.sum(kept * drift, axis=0, keepdims=True))
    y_ref[0, TAIL:, :] = small_rows(d_ref, norms)


def query_kernel(
    d_ref, q_ref, v_ref, w_ref, fk_ref, fq_ref, oq_ref, pr_ref, sc_ref, dr_ref, s_ref,
    qg_ref, gk_ref, vl_ref, wq_ref,
):
    mask = pair_mask(d_ref)
    head = head_rows(d_ref)
    total = jnp.zeros((DH, F), F32)
    for a in range(PAIR):
        scaled = sc_ref[:, cols(a)]
        drift = dr_ref[a]
        score = dot(scaled, v_ref[:, cols(a)], (1, 1)) + drift
        dprobs = jnp.where(mask, score, 0.0).astype(BF16)
        state = s_ref[0, a * F : (a + 1) * F, :].astype(BF16)
        far = dot(scaled, state, (1, 1)) + norm_row(s_ref, a) * drift
        grad_fq = dot(dprobs, fk_ref[a], (1, 0)) + jnp.where(head, far, 0.0)
        grad_pq = (grad_fq * oq_ref[a]).astype(BF16)
        qg_ref[:, cols(a)] = dot(grad_pq, w_ref[...], (1, 1))
        total = total + dot(q_ref[:, cols(a)], grad_pq, (0, 0))
        gk_ref[a] = dot(dprobs, fq_ref[a], (0, 0))
        vl_ref[:, cols(a)] = dot(pr_ref[a], scaled, (0, 0))

    @pl.when(pl.program_id(0) == 0)
    def _():
        wq_ref[...] = total

    @pl.when(pl.program_id(0) != 0)
    def _():
        wq_ref[...] += total


def grad_kernel(
    d_ref, k_ref, v_ref, w_ref, fk_ref, ok_ref, gk_ref, vl_ref, s_ref, wq_ref,
    kg_ref, vg_ref, wk_ref,
):
    tail = tail_rows(d_ref)
    total = jnp.zeros((DH, F), F32)
    for a in range(PAIR):
        state = s_ref[0, a * F : (a + 1) * F, :].astype(BF16)
        far = dot(v_ref[:, cols(a)], state, (1, 1)) + norm_row(s_ref, a)
        grad_fk = gk_ref[a] + jnp.where(tail, far, 0.0)
        grad_pk = (grad_fk * ok_ref[a]).astype(BF16)
        kg_ref[:, cols(a)] = dot(grad_pk, w_ref[...], (1, 1))
        total = total + dot(k_ref[:, cols(a)], grad_pk, (0, 0))
        vg_ref[:, cols(a)] = vl_ref[:, cols(a)] + jnp.where(
            tail, dot(fk_ref[a], state, (1, 0)), 0.0
        )

    @pl.when(pl.program_id(0) == 0)
    def _():
        wk_ref[...] = wq_ref[...] + total

    @pl.when(pl.program_id(0) != 0)
    def _():
        wk_ref[...] += total


def tile(ref, i, row):
    return jnp.broadcast_to(ref[i, row : row + 1, :], (8, DH))


def total_kernel(reverse, z_ref, r_ref):
    row = FIRST if reverse else LAST
    edge = 0 if reverse else GROUP - 1
    keep = [tile(z_ref, i, row) == tile(z_ref, edge, row) for i in range(GROUP)]

    def step(n, _):
        at = pl.ds(pl.multiple_of(n * 8, 8), 8)
        total = z_ref[edge, at, :]
        for i in range(GROUP):
            if i != edge:
                total = total + jnp.where(keep[i], z_ref[i, at, :], 0.0)
        r_ref[at, :] = total
        return 0

    lax.fori_loop(0, TAIL // 8, step, 0)
    small = z_ref[edge, TAIL:, :]
    for i in range(GROUP):
        if i != edge:
            small = small + jnp.where(keep[i], z_ref[i, TAIL:, :], 0.0)
    index = lax.broadcasted_iota(jnp.int32, (8, DH), 0)
    r_ref[TAIL:, :] = jnp.where(index < 2 * PAIR, small, tile(z_ref, edge, row))


def carry_kernel(reverse, z_ref, a_ref, b_ref, c_ref, e_ref, s_ref):
    enter, leave = (LAST, FIRST) if reverse else (FIRST, LAST)
    order = list(range(GROUP))[::-1] if reverse else list(range(GROUP))
    far = (a_ref, b_ref, c_ref, e_ref)
    door = tile(z_ref, order[0], enter)
    keep_far = [jnp.broadcast_to(ref[LAST : LAST + 1, :], (8, DH)) == door for ref in far]
    through = [tile(z_ref, i, enter) == tile(z_ref, i, leave) for i in order]
    joined = [
        tile(z_ref, order[n + 1], enter) == tile(z_ref, order[n], leave) for n in range(GROUP - 1)
    ]

    def step(n, _):
        at = pl.ds(pl.multiple_of(n * 8, 8), 8)
        state = jnp.zeros((8, DH), F32)
        for keep, ref in zip(keep_far, far):
            state = state + jnp.where(keep, ref[at, :], 0.0)
        s_ref[order[0], at, :] = state
        for m in range(GROUP - 1):
            state = z_ref[order[m], at, :] + jnp.where(through[m], state, 0.0)
            state = jnp.where(joined[m], state, 0.0)
            s_ref[order[m + 1], at, :] = state
        return 0

    lax.fori_loop(0, ROWS // 8, step, 0)


def groups(count, stride, inner):
    block = stride * inner
    return [
        [base + offset + stride * i for i in range(inner)]
        for base in range(0, count, block)
        for offset in range(stride)
    ]


def whole(shape):
    return pl.BlockSpec(shape, lambda i: (0,) * len(shape))


def exchange(packed, reverse):
    count = lax.axis_size("ctx")
    near = groups(count, 1, GROUP)
    held = lax.all_to_all(packed, "ctx", 0, 0, axis_index_groups=near)
    total = pl.pallas_call(
        lambda *refs: total_kernel(reverse, *refs),
        out_shape=jax.ShapeDtypeStruct((ROWS, DH), F32),
        name="total_back" if reverse else "total",
    )(held)
    got = []
    for n in range(1, REACH + 1):
        by = -GROUP * n if reverse else GROUP * n
        pairs = [(i, i + by) for i in range(count) if 0 <= i + by < count]
        got.append(lax.ppermute(total, "ctx", pairs))
    states = pl.pallas_call(
        lambda *refs: carry_kernel(reverse, *refs),
        out_shape=jax.ShapeDtypeStruct((GROUP, ROWS, DH), F32),
        name="carry_back" if reverse else "carry",
    )(held, *got)
    return lax.all_to_all(states, "ctx", 0, 0, axis_index_groups=near)


def reduced(part):
    count = lax.axis_size("ctx")
    both = lax.axis_size("dp")
    near = groups(count, 1, GROUP)
    rows = DH // GROUP
    piece = jnp.sum(
        lax.all_to_all(part.reshape(GROUP, rows, F), "ctx", 0, 0, axis_index_groups=near), axis=0
    )
    others = count // GROUP
    far = [
        [d * count + p + GROUP * i for d in range(both) for i in range(others)] for p in range(GROUP)
    ]
    spread = jnp.broadcast_to(piece[None], (both * others, rows, F))
    piece = jnp.sum(
        lax.all_to_all(spread, ("dp", "ctx"), 0, 0, axis_index_groups=far), axis=0
    )
    spread = jnp.broadcast_to(piece[None], (GROUP, rows, F))
    return lax.all_to_all(spread, "ctx", 0, 0, axis_index_groups=near).reshape(DH, F)


def shards(queries, keys, values, doc_ids, feat_weight, out_grad):
    query, key, value, grad = (x.reshape(T, H * DH) for x in (queries, keys, values, out_grad))
    docs = pl.BlockSpec(memory_space=pltpu.SMEM)
    wide = pl.BlockSpec((T, PAIR * DH), lambda i: (0, i))
    weight = whole((DH, F))
    feats = pl.BlockSpec((PAIR, T, F), lambda i: (i, 0, 0))
    square = pl.BlockSpec((PAIR, T, T), lambda i: (i, 0, 0))
    column = pl.BlockSpec((PAIR, T, 1), lambda i: (i, 0, 0))
    packed = pl.BlockSpec((1, ROWS, DH), lambda i: (i, 0, 0))
    wide_f = jax.ShapeDtypeStruct((T, H * DH), F32)
    wide_b = jax.ShapeDtypeStruct((T, H * DH), BF16)
    feats_f = jax.ShapeDtypeStruct((H, T, F), F32)
    feats_b = jax.ShapeDtypeStruct((H, T, F), BF16)
    square_b = jax.ShapeDtypeStruct((H, T, T), BF16)
    column_f = jax.ShapeDtypeStruct((H, T, 1), F32)
    packed_f = jax.ShapeDtypeStruct((GROUP, ROWS, DH), F32)
    weight_f = jax.ShapeDtypeStruct((DH, F), F32)

    def call(kernel, name, in_specs, out_specs, out_shape):
        return pl.pallas_call(
            kernel,
            grid=(GROUP,),
            in_specs=[docs] + in_specs,
            out_specs=out_specs,
            out_shape=out_shape,
            name=name,
        )

    sent, feat_k, one_k = call(
        key_kernel, "keys", [wide, wide, weight], [packed, feats, feats], [packed_f, feats_b, feats_f]
    )(doc_ids, key, value, feat_weight)
    feat_q, one_q, probs, num, den = call(
        local_kernel,
        "local",
        [wide, wide, weight, feats],
        [feats, feats, square, wide, column],
        [feats_b, feats_f, square_b, wide_f, column_f],
    )(doc_ids, query, value, feat_weight, feat_k)
    state = exchange(sent, False)
    sent, out, scaled, drift = call(
        out_kernel,
        "output",
        [feats, wide, column, wide, packed],
        [packed, wide, wide, column],
        [packed_f, wide_f, wide_b, column_f],
    )(doc_ids, feat_q, num, den, grad, state)
    query_grad, grad_k, value_part, weight_q = call(
        query_kernel,
        "query",
        [wide, wide, weight, feats, feats, feats, square, wide, column, packed],
        [wide, feats, wide, weight],
        [wide_f, feats_f, wide_f, weight_f],
    )(doc_ids, query, value, feat_weight, feat_k, feat_q, one_q, probs, scaled, drift, state)
    adjoint = exchange(sent, True)
    key_grad, value_grad, part = call(
        grad_kernel,
        "grads",
        [wide, wide, weight, feats, feats, feats, wide, packed, weight],
        [wide, wide, weight],
        [wide_f, wide_f, weight_f],
    )(doc_ids, key, value, feat_weight, feat_k, one_k, grad_k, value_part, adjoint, weight_q)
    weight_grad = reduced(part)
    scale = lax.rsqrt(jnp.mean(weight_grad * weight_grad) + EPSILON)
    new_weight = feat_weight.astype(F32) - RATE * weight_grad * scale
    shape_out = (1, T, H * DH)
    return (
        out.reshape(shape_out),
        query_grad.reshape(shape_out),
        key_grad.reshape(shape_out),
        value_grad.reshape(shape_out),
        new_weight,
    )


def solution(mesh):
    split = P("dp", "ctx", None)
    return jax.shard_map(
        shards,
        mesh=mesh,
        in_specs=(split, split, split, P("dp", "ctx"), P(), split),
        out_specs=(split, split, split, split, P()),
        check_vma=False,
    )
```
